32 devices in a mesh: tm: 2 (over core), space: 16 (over z, y, x).
Axes of the slice: x: 2, y: 2, z: 4, core: 2. Of those that a mesh axis runs over, the one named last changes fastest.
Arguments:
- forcing: float32 [2, 4, 4, 8, 64, 640], P('tm', None, None, None, 'space'), may hold values from -6 to 6
- trajectory: float32 [2, 2, 8, 64, 640], P('tm', None, None, 'space'), may hold values from -0.45 to 0.45
- land_mask: int32 [8, 64, 640], P(None, 'space'), may hold values 0 or 1
- coupling: float32 [4, 4], replicated, may hold values from -0.6 to 0.6
Outputs:
- increments: float32 [2, 4, 4, 8, 64, 640], P('tm', None, None, None, 'space')
The draws below stay inside these ranges and needn't reach their ends.
All inputs are finite; a program needn't handle non-finite values. No bound on the sum of `land_mask` on one device may be relied on, other than what follows from the above.
Results may differ from the reference program's by a relative error of at most 0.0001.
Values sent between devices are 32-bit elements; how exact they have to be, the bound alone decides.
No kernel may reach another device: no remote copies, remote signals or barrier semaphores. Data moves between devices by JAX's collectives and lax.ppermute only.
A program may use at most 64 MiB of HBM per device.

```python
import jax
import jax.numpy as jnp
from jax import lax

MEM = 4
VAR = 4
LEV = 8
LAT = 640
STEPS = 2
SUB = 2
NLON = 64


def place_ends(entries, own_key, least, largest):
    longest = entries.shape.index(max(entries.shape))
    spots = []
    for shift in (0, 1):
        where = [jax.random.randint(jax.random.fold_in(own_key, axis), (), 0, length) for axis, length in enumerate(entries.shape)]
        where[longest] = (where[longest] + shift) % entries.shape[longest]
        spots.append(tuple(where))
    return entries.at[spots[0]].set(least).at[spots[1]].set(largest)


def levels(rng, extent, shards, least, high):
    loudness, own = 1.0, jax.random.fold_in(rng, 6)
    for dim, blocks in shards:
        draws = jnp.exp(jax.random.uniform(jax.random.fold_in(own, dim), (blocks,), jnp.float32, least / len(shards), high / len(shards)))
        loudness = loudness * jnp.repeat(draws, extent[dim] // blocks).reshape([-1 if axis == dim else 1 for axis in range(len(extent))])
    return loudness


def centred(key, shape, spread, limit, split=(), kind=jnp.bfloat16):
    loudness = levels(key, shape, split, -0.22, 0.18) if split else 1.0
    array = jax.random.normal(key, shape, jnp.float32) * spread * loudness
    return jnp.minimum(jnp.maximum(array, -limit), limit).astype(kind)


def setup_inputs(seed: int = 0) -> dict:
    seeds = jax.random.split(jax.random.key(seed), 5)
    forcing = centred(seeds[0], (SUB, MEM, VAR, LEV, NLON, LAT), 1.0, 6.0, ((0, 2), (4, 16)), jnp.float32)
    trajectory = jnp.clip(jax.random.uniform(seeds[1], (SUB, 2, LEV, NLON, LAT), jnp.float32, -0.45, 0.45) * levels(seeds[1], (SUB, 2, LEV, NLON, LAT), ((0, 2), (3, 16)), -0.4, 0.0), -0.45, 0.45)
    land_mask = place_ends((jax.random.randint(seeds[2], (LEV, NLON, LAT), 0, 4) < 3).astype(jnp.int32), jax.random.fold_in(seeds[2], 1), 0, 1)
    coupling = centred(seeds[3], (VAR, VAR), 0.15, 0.6, (), jnp.float32)
    return {"forcing": forcing, "trajectory": trajectory, "land_mask": land_mask, "coupling": coupling}


def tendency(center, east, west, upper, lower, wind_u, wind_v, damping, coupling):
    mixed = jnp.einsum("cd,mdlij->mclij", coupling, center, precision=lax.Precision.HIGHEST)
    advect = -wind_u * (east - west) * 0.5 - wind_v * (upper - lower) * 0.5
    return center + (advect + damping * (east + west + upper + lower - 4.0 * center) + mixed)


def lat_shifts(center):
    widths = ((0, 0),) * 4
    upper = jnp.pad(center[..., 1:], widths + ((0, 1),))
    lower = jnp.pad(center[..., :-1], widths + ((1, 0),))
    return upper, lower


def model_step(field, wind_u, wind_v, damping, coupling):
    east = jnp.roll(field, -1, axis=3)
    west = jnp.roll(field, 1, axis=3)
    upper, lower = lat_shifts(field)
    return tendency(field, east, west, upper, lower, wind_u, wind_v, damping, coupling)


def reference(forcing, trajectory, land_mask, coupling):
    damping = 0.15 * land_mask.astype(jnp.float32)
    state = forcing[0]
    results = [state]
    for window in range(1, SUB):
        wind_u = trajectory[window - 1, 0]
        wind_v = trajectory[window - 1, 1]
        for step in range(STEPS):
            state = model_step(state, wind_u, wind_v, damping, coupling)
        state = state + forcing[window]
        results.append(state)
    return jnp.stack(results)
```

```python
import functools
import math

import jax
import jax.numpy as jnp
from jax import lax
from jax.experimental import pallas as pl
from jax.experimental.pallas import tpu as pltpu
from jax.sharding import PartitionSpec as P


STEPS = 2
HBM = pl.BlockSpec(memory_space=pltpu.HBM)
VMEM = pl.BlockSpec(memory_space=pltpu.VMEM)
SMEM = pl.BlockSpec(memory_space=pltpu.SMEM)


def run_copies(pairs, sem):
    copies = [pltpu.make_async_copy(src, dst, sem.at[i]) for i, (src, dst) in enumerate(pairs)]
    for copy in copies:
        copy.start()
    return copies


def wait_all(copies):
    for copy in copies:
        copy.wait()


def is_even():
    return lax.rem(lax.axis_index("space"), 2) == 0


def shifts(x):
    width = x.shape[-1]
    return pltpu.roll(x, width - 1, 1), pltpu.roll(x, 1, 1)


def stencil(u, v, mask):
    nu = 0.15 * mask.astype(jnp.float32)
    u, v = 0.5 * u, 0.5 * v
    lat = lax.broadcasted_iota(jnp.int32, u.shape, 1)
    north = jnp.where(lat == u.shape[1] - 1, 0.0, nu - v)
    south = jnp.where(lat == 0, 0.0, nu + v)
    return 1.0 - 4.0 * nu, nu - u, nu + u, north, south


def edges_kernel(hop, x, traj, mask, near, far, wind, open_, sem):
    last = x.shape[1] - 1
    rows, lev = x.shape[0], traj.shape[1]

    def send(j_near, j_far):
        copies = run_copies(
            [
                (x.at[:, j_near, :], near.at[0:rows, :]),
                (x.at[:, j_far, :], far.at[0:rows, :]),
                (traj.at[0, :, 0, :], wind.at[0]),
                (traj.at[0, :, last, :], wind.at[1]),
                (mask.at[:, 0, :], open_.at[0]),
                (mask.at[:, last, :], open_.at[1]),
            ],
            sem,
        )
        wait_all(copies[2:])
        for j, ref in ((j_near, near), (j_far, far)):
            side = 0 if j == 0 else 1
            nu = 0.15 * open_[side].astype(jnp.float32)
            half = 0.5 * wind[side]
            ref[rows : rows + lev, :] = nu + half if j == 0 else nu - half
        wait_all(copies[:2])

    @pl.when(lax.axis_index("tm") == hop)
    def _():
        even = is_even()
        pl.when(even)(lambda: send(last, 0))
        pl.when(jnp.logical_not(even))(lambda: send(0, last))


def load_coefs(traj, mask, wind, open_, sem):
    lon = mask.shape[1]
    pairs = []
    for j in range(lon):
        pairs.append((traj.at[0, :, j, :], wind.at[0, j]))
        pairs.append((traj.at[1, :, j, :], wind.at[1, j]))
        pairs.append((mask.at[:, j, :], open_.at[j]))
    return run_copies(pairs, sem)


def partial_kernel(hop, var, x, traj, mask, coupling, near, far, xs, wind, open_, sem_x, sem_c):
    lon = x.shape[1]
    rows, lev = x.shape[0], traj.shape[1]
    last = lon - 1

    @pl.when(lax.axis_index("tm") == hop)
    def _():
        loads = run_copies([(x.at[:, j, :], xs.at[j]) for j in range(lon)], sem_x)
        wait_all(load_coefs(traj, mask, wind, open_, sem_c))
        wait_all(loads)

        def send(j_near, j_far):
            for j, out in ((j_near, near), (j_far, far)):
                inner = 1 if j == 0 else last - 1
                mid, east, west, north, south = stencil(wind[0, j], wind[1, j], open_[j])
                side = east if j == 0 else west

                def member(m, carry):
                    base = pl.multiple_of(m * var * lev, lev)
                    block = [xs[j, pl.ds(base + d * lev, lev), :] for d in range(var)]
                    for c in range(var):
                        up, low = shifts(block[c])
                        total = mid * block[c] + side * xs[inner, pl.ds(base + c * lev, lev), :]
                        total += north * up + south * low
                        for d in range(var):
                            total += coupling[c, d] * block[d]
                        out[pl.ds(base + c * lev, lev), :] = total
                    return carry

                lax.fori_loop(0, rows // (var * lev), member, 0)

        even = is_even()
        pl.when(even)(lambda: send(last, 0))
        pl.when(jnp.logical_not(even))(lambda: send(0, last))


def main_kernel(
    hop, var, own, sent, traj, mask, coupling, near, far, z, edge,
    xs, ss, halo, coef, force, wind, open_, sem_o, sem_x, sem_c, sem_h,
):
    rows, lon = own.shape[0], own.shape[1]
    lev = traj.shape[1]
    last = lon - 1
    receiver = lax.axis_index("tm") == hop + 1

    @pl.when(jnp.logical_not(receiver))
    def _():
        wait_all(run_copies([(own.at[:, j, :], z.at[j]) for j in range(lon)], sem_o))

    @pl.when(receiver)
    def _():
        loads = run_copies([(sent.at[:, j, :], xs.at[j]) for j in range(lon)], sem_x)
        coefs = load_coefs(traj, mask, wind, open_, sem_c)
        forces = run_copies([(own.at[:, j, :], force.at[j]) for j in range(lon)], sem_o)
        even = is_even()

        @pl.when(even)
        def _():
            wait_all(run_copies([(far, halo.at[0]), (near, halo.at[1])], sem_h))

        @pl.when(jnp.logical_not(even))
        def _():
            wait_all(run_copies([(near, halo.at[0]), (far, halo.at[1])], sem_h))

        wait_all(coefs)
        for j in range(lon):
            for k, value in enumerate(stencil(wind[0, j], wind[1, j], open_[j])):
                coef[k, j] = value
        edge[0] = coef[2, 0]
        edge[1] = coef[1, last]
        wait_all(loads)
        wait_all(forces)

        def step(j, centre, east, west, skip_e=False, skip_w=False):
            block = [centre(d) for d in range(var)]
            for c in range(var):
                up, low = shifts(block[c])
                total = coef[0, j] * block[c] + coef[3, j] * up + coef[4, j] * low
                if not skip_e:
                    total += coef[1, j] * east(c)
                if not skip_w:
                    total += coef[2, j] * west(c)
                for d in range(var):
                    total += coupling[c, d] * block[d]
                yield c, total

        def member(m, carry):
            base = pl.multiple_of(m * var * lev, lev)

            def at(ref, j):
                return lambda d: ref[j, pl.ds(base + d * lev, lev), :]

            for j in range(lon):
                east = at(xs, j + 1) if j < last else at(halo, 1)
                west = at(xs, j - 1) if j > 0 else at(halo, 0)
                for c, total in step(j, at(xs, j), east, west):
                    ss[j, pl.ds(base + c * lev, lev), :] = total
            weight = (
                coef[2, 0] * halo[0, rows : rows + lev, :],
                coef[1, last] * halo[1, rows : rows + lev, :],
            )
            for j in range(lon):
                east = at(ss, j + 1) if j < last else None
                west = at(ss, j - 1) if j > 0 else None
                for c, total in step(j, at(ss, j), east, west, j == last, j == 0):
                    total += at(force, j)(c)
                    if j == 0:
                        total += weight[0] * at(xs, j)(c)
                    if j == last:
                        total += weight[1] * at(xs, j)(c)
                    z[j, pl.ds(base + c * lev, lev), :] = total
            return carry

        lax.fori_loop(0, rows // (var * lev), member, 0)


def finish_kernel(hop, near, far, z, edge, out, done, sem):
    lon, rows = z.shape[0], z.shape[1]
    lev = edge.shape[1]
    last = lon - 1
    receiver = lax.axis_index("tm") == hop + 1

    @pl.when(jnp.logical_not(receiver))
    def _():
        wait_all(run_copies([(z.at[j], out.at[:, j, :]) for j in range(lon)], sem))

    @pl.when(receiver)
    def _():
        even = is_even()

        def finish(j_near, j_far):
            copies = [pltpu.make_async_copy(z.at[j], out.at[:, j, :], sem.at[j]) for j in range(1, last)]
            for copy in copies:
                copy.start()
            for j, ref in ((j_near, near), (j_far, far)):
                side = 0 if j == 0 else 1
                for r in range(0, rows, lev):
                    done[side, r : r + lev, :] = z[j, r : r + lev, :] + edge[side] * ref[r : r + lev, :]
                copy = pltpu.make_async_copy(done.at[side], out.at[:, j, :], sem.at[j])
                copy.start()
                copies.append(copy)
            wait_all(copies)

        pl.when(even)(lambda: finish(last, 0))
        pl.when(jnp.logical_not(even))(lambda: finish(0, last))


def call(kernel, out_shape, in_specs, out_specs, scratch, semaphores):
    room = sum(4 * math.prod(ref.inner_aval.shape) for ref in scratch)
    return pl.pallas_call(
        kernel,
        out_shape=out_shape,
        in_specs=in_specs,
        out_specs=out_specs,
        scratch_shapes=scratch + [pltpu.SemaphoreType.DMA((count,)) for count in semaphores],
        compiler_params=pltpu.CompilerParams(vmem_limit_bytes=room + 2**22),
    )


def advance(hop, state, traj, land_mask, coupling, var):
    rows, lon, lat = state.shape
    lev = traj.shape[1]
    n = lax.axis_size("space")
    f32 = jnp.float32

    def buffer(*dims, dtype=f32):
        return pltpu.VMEM(dims, dtype)

    def moved(block, move):
        pairs = [(hop * n + s, (hop + 1) * n + move(s) % n) for s in range(n)]
        block = lax.ppermute(block, ("tm", "space"), pairs)
        return pltpu.with_memory_space_constraint(block, pltpu.VMEM)

    def to_near(s):
        return s + 1 if s % 2 == 0 else s - 1

    def to_far(s):
        return s - 1 if s % 2 == 0 else s + 1

    held = [pltpu.with_memory_space_constraint(a, pltpu.HBM) for a in (state, traj, land_mask)]
    near, far = call(
        functools.partial(edges_kernel, hop),
        [buffer(rows + lev, lat)] * 2,
        [HBM] * 3,
        [VMEM] * 2,
        [buffer(2, lev, lat), buffer(2, lev, lat, dtype=jnp.int32)],
        [6],
    )(*held)
    near_x = moved(near, to_near)
    far_x = moved(far, to_far)
    near, far = call(
        functools.partial(partial_kernel, hop, var),
        [buffer(rows, lat)] * 2,
        [HBM] * 3 + [SMEM],
        [VMEM] * 2,
        [buffer(lon, rows, lat), buffer(2, lon, lev, lat), buffer(lon, lev, lat, dtype=jnp.int32)],
        [lon, 3 * lon],
    )(*held, coupling)
    near_p = moved(near, to_near)
    far_p = moved(far, to_far)
    sent = moved(state, lambda s: s)
    sent_traj = moved(traj, lambda s: s)
    z, edge = call(
        functools.partial(main_kernel, hop, var),
        [buffer(lon, rows, lat), buffer(2, lev, lat)],
        [HBM, VMEM, VMEM, HBM, SMEM, VMEM, VMEM],
        [VMEM] * 2,
        [
            buffer(lon, rows, lat),
            buffer(lon, rows, lat),
            buffer(2, rows + lev, lat),
            buffer(5, lon, lev, lat),
            buffer(lon, rows, lat),
            buffer(2, lon, lev, lat),
            buffer(lon, lev, lat, dtype=jnp.int32),
        ],
        [lon, lon, 3 * lon, 2],
    )(held[0], sent, sent_traj, held[2], coupling, near_x, far_x)
    return call(
        functools.partial(finish_kernel, hop),
        jax.ShapeDtypeStruct(state.shape, f32),
        [VMEM] * 4,
        HBM,
        [buffer(2, rows, lat)],
        [lon],
    )(near_p, far_p, z, edge)


def per_device(forcing, trajectory, land_mask, coupling):
    _, mem, var, lev, lon, lat = forcing.shape
    assert lax.axis_size("space") % 2 == 0 and lon >= 2 and STEPS == 2
    state = forcing.reshape(mem * var * lev, lon, lat)
    for hop in range(lax.axis_size("tm") - 1):
        state = advance(hop, state, trajectory[0], land_mask, coupling, var)
    return state.reshape(forcing.shape)


def solution(mesh):
    return jax.shard_map(
        per_device,
        mesh=mesh,
        in_specs=(
            P("tm", None, None, None, "space", None),
            P("tm", None, None, "space", None),
            P(None, "space", None),
            P(),
        ),
        out_specs=P("tm", None, None, None, "space", None),
        check_vma=False,
    )
```

```python
import functools
import math

import jax
import jax.numpy as jnp
from jax import lax
from jax.experimental import pallas as pl
from jax.experimental.pallas import tpu as pltpu
from jax.sharding import PartitionSpec as P


STEPS = 2
HBM = pl.BlockSpec(memory_space=pltpu.HBM)
VMEM = pl.BlockSpec(memory_space=pltpu.VMEM)


def run_copies(pairs, sem):
    copies = [pltpu.make_async_copy(src, dst, sem.at[i]) for i, (src, dst) in enumerate(pairs)]
    for copy in copies:
        copy.start()
    return copies


def wait_all(copies):
    for copy in copies:
        copy.wait()


def by_parity(body, last):
    even = lax.rem(lax.axis_index("space"), 2) == 0
    pl.when(even)(lambda: body(last, 0))
    pl.when(jnp.logical_not(even))(lambda: body(0, last))


def shifts(x):
    return pltpu.roll(x, x.shape[-1] - 1, 1), pltpu.roll(x, 1, 1)


def stencil(u, v, nu):
    u, v = 0.5 * u, 0.5 * v
    lat = lax.broadcasted_iota(jnp.int32, u.shape, 1)
    north = jnp.where(lat == u.shape[1] - 1, 0.0, nu - v)
    south = jnp.where(lat == 0, 0.0, nu + v)
    return 1.0 - 4.0 * nu, nu - u, nu + u, north, south


def spread(coupling, shape):
    var = coupling.shape[0]
    table = coupling[...]
    return [[jnp.broadcast_to(table[c : c + 1, d : d + 1], shape) for d in range(var)] for c in range(var)]


def mix(pair, block, c):
    width = block[0].shape[1] // pair[c][0].shape[1]
    total = None
    for d, field in enumerate(block):
        term = jnp.tile(pair[c][d], (1, width)) * field
        total = term if total is None else total + term
    return total


class Packed:
    def __init__(self, ref, j, rows, lev):
        self.ref, self.j, self.rows, self.lev = ref, j, rows, lev

    def field(self, base):
        return self.ref[self.j, pl.ds(base, self.lev), :]

    def weights(self):
        u, v, nu = (self.ref[self.j, self.rows + k * self.lev : self.rows + (k + 1) * self.lev, :] for k in range(3))
        return stencil(u, v, nu)


def edges_kernel(hop, x, traj, mask, near, far, packed, open_, sem):
    rows, lon = x.shape[0], x.shape[1]
    lev = traj.shape[1]
    last = lon - 1

    @pl.when(lax.axis_index("tm") == hop)
    def _():
        fields = [(x.at[:, j, :], packed.at[j, 0:rows, :]) for j in (0, last, *range(1, last))]
        others = []
        for j in range(lon):
            for k in range(2):
                start = rows + k * lev
                others.append((traj.at[k, :, j, :], packed.at[j, start : start + lev, :]))
            others.append((mask.at[:, j, :], open_.at[j]))
        copies = run_copies(fields[:2] + others + fields[2:], sem)
        wait_all(copies[2 : 2 + len(others)])
        for j in range(lon):
            packed[j, rows + 2 * lev :, :] = 0.15 * open_[j].astype(jnp.float32)
        wait_all(copies[:2])

        def fill(j_near, j_far):
            for j, ref in ((j_near, near), (j_far, far)):
                _, east, west, _, _ = Packed(packed, j, rows, lev).weights()
                for r in range(0, rows, lev):
                    ref[r : r + lev, :] = packed[j, r : r + lev, :]
                ref[rows:, :] = west if j == 0 else east

        by_parity(fill, last)
        wait_all(copies[2 + len(others) :])


def partial_kernel(hop, packed, coupling, near, far):
    last = packed.shape[0] - 1
    rows, var = near.shape[0], coupling.shape[0]
    lev = (packed.shape[1] - rows) // 3

    @pl.when(lax.axis_index("tm") == hop)
    def _():
        pair = spread(coupling, (lev, 128))

        def send(j_near, j_far):
            for j, out in ((j_far, far), (j_near, near)):
                here = Packed(packed, j, rows, lev)
                inner = Packed(packed, 1 if j == 0 else last - 1, rows, lev)
                mid, east, west, north, south = here.weights()
                side = east if j == 0 else west

                def member(m, carry):
                    base = pl.multiple_of(m * var * lev, lev)
                    block = [here.field(base + d * lev) for d in range(var)]
                    for c in range(var):
                        up, low = shifts(block[c])
                        total = mid * block[c] + side * inner.field(base + c * lev)
                        total += north * up + south * low
                        out[pl.ds(base + c * lev, lev), :] = total + mix(pair, block, c)
                    return carry

                lax.fori_loop(0, rows // (var * lev), member, 0)

        by_parity(send, last)


def main_kernel(hop, own, packed, sent, coupling, near, far, out, z, edge, ss, halo, coef, force, sem_o, sem_h):
    rows, lon = own.shape[0], own.shape[1]
    var = coupling.shape[0]
    lev = (sent.shape[1] - rows) // 3
    last = lon - 1
    row = lax.axis_index("tm")

    @pl.when(row == hop)
    def _():
        wait_all(run_copies([(packed.at[j, 0:rows, :], out.at[:, j, :]) for j in range(lon)], sem_o))

    @pl.when(jnp.logical_and(row != hop, row != hop + 1))
    def _():
        wait_all(run_copies([(own.at[:, j, :], force.at[j]) for j in range(lon)], sem_o))
        wait_all(run_copies([(force.at[j], out.at[:, j, :]) for j in range(lon)], sem_o))

    @pl.when(row == hop + 1)
    def _():
        forces = run_copies([(own.at[:, j, :], force.at[j]) for j in range(lon)], sem_o)

        def fill(j_near, j_far):
            pairs = [(ref, halo.at[0 if j == 0 else 1]) for j, ref in ((j_near, near), (j_far, far))]
            wait_all(run_copies(pairs, sem_h))

        by_parity(fill, last)
        for j in range(lon):
            for k, value in enumerate(Packed(sent, j, rows, lev).weights()):
                coef[k, j] = value
        edge[0] = coef[2, 0]
        edge[1] = coef[1, last]
        pair = spread(coupling, (lev, 128))

        def at(ref, j, base):
            return lambda d: ref[j, pl.ds(base + d * lev, lev), :]

        def step(j, centre, east, west):
            block = [centre(d) for d in range(var)]
            for c in range(var):
                up, low = shifts(block[c])
                total = coef[0, j] * block[c] + coef[3, j] * up + coef[4, j] * low
                if east is not None:
                    total += coef[1, j] * east(c)
                if west is not None:
                    total += coef[2, j] * west(c)
                yield c, total + mix(pair, block, c)

        def first(m, carry):
            base = pl.multiple_of(m * var * lev, lev)
            for j in range(lon):
                east = at(sent, j + 1, base) if j < last else at(halo, 1, base)
                west = at(sent, j - 1, base) if j > 0 else at(halo, 0, base)
                for c, total in step(j, at(sent, j, base), east, west):
                    ss[j, pl.ds(base + c * lev, lev), :] = total
            return carry

        members = rows // (var * lev)
        lax.fori_loop(0, members, first, 0)
        wait_all(forces)

        def second(m, carry):
            base = pl.multiple_of(m * var * lev, lev)
            weight = {0: coef[2, 0] * halo[0, rows:, :], last: coef[1, last] * halo[1, rows:, :]}
            for j in range(lon):
                east = at(ss, j + 1, base) if j < last else None
                west = at(ss, j - 1, base) if j > 0 else None
                for c, total in step(j, at(ss, j, base), east, west):
                    total += at(force, j, base)(c)
                    if j in weight:
                        total += weight[j] * at(sent, j, base)(c)
                    z[j, pl.ds(base + c * lev, lev), :] = total
            return carry

        lax.fori_loop(0, members, second, 0)


def finish_kernel(hop, whole, block, z, edge, out_in, out, done, sem):
    del out_in
    lon, rows = z.shape[0], z.shape[1]
    lev = edge.shape[1]
    last = lon - 1

    @pl.when(lax.axis_index("tm") == hop + 1)
    def _():
        copies = []
        if whole:
            copies = run_copies([(z.at[j], out.at[:, j, :]) for j in range(1, last)], sem)

        def finish(j_near, j_far):
            j = j_far if whole else j_near
            weight = edge[0 if j == 0 else 1]
            for r in range(0, rows, lev):
                done[r : r + lev, :] = z[j, r : r + lev, :] + weight * block[r : r + lev, :]
            copy = pltpu.make_async_copy(done, out.at[:, j, :], sem.at[last])
            copy.start()
            copy.wait()

        by_parity(finish, last)
        wait_all(copies)


def call(kernel, out_shape, in_specs, out_specs, scratch, semaphores, aliases=None):
    room = sum(4 * math.prod(ref.inner_aval.shape) for ref in scratch)
    return pl.pallas_call(
        kernel,
        out_shape=out_shape,
        in_specs=in_specs,
        out_specs=out_specs,
        scratch_shapes=scratch + [pltpu.SemaphoreType.DMA((count,)) for count in semaphores],
        compiler_params=pltpu.CompilerParams(vmem_limit_bytes=room + 2**22),
        input_output_aliases=aliases or {},
    )


def advance(hop, state, traj, land_mask, coupling):
    rows, lon, lat = state.shape
    lev = traj.shape[1]
    n = lax.axis_size("space")
    f32 = jnp.float32

    def buffer(*dims, dtype=f32):
        return pltpu.VMEM(dims, dtype)

    def in_vmem(array):
        return pltpu.with_memory_space_constraint(array, pltpu.VMEM)

    def in_hbm(array):
        return pltpu.with_memory_space_constraint(array, pltpu.HBM)

    def moved(block, move):
        pairs = [(hop * n + s, (hop + 1) * n + move(s) % n) for s in range(n)]
        block = lax.ppermute(block, ("tm", "space"), pairs)
        return in_vmem(block)

    def to_near(s):
        return s + 1 if s % 2 == 0 else s - 1

    def to_far(s):
        return s - 1 if s % 2 == 0 else s + 1

    coupling = in_vmem(coupling)
    near, far, packed = call(
        functools.partial(edges_kernel, hop),
        [buffer(rows + lev, lat)] * 2 + [buffer(lon, rows + 3 * lev, lat)],
        [HBM] * 3,
        [VMEM] * 3,
        [buffer(lon, lev, lat, dtype=jnp.int32)],
        [4 * lon],
    )(in_hbm(state), in_hbm(traj), in_hbm(land_mask))
    near_x = moved(near, to_near)
    far_x = moved(far, to_far)
    sent = moved(packed, lambda s: s)
    packed = in_vmem(packed)
    near, far = call(
        functools.partial(partial_kernel, hop),
        [buffer(rows, lat)] * 2,
        [VMEM] * 2,
        [VMEM] * 2,
        [],
        [],
    )(packed, coupling)
    far_p = moved(far, to_far)
    near_p = moved(near, to_near)
    out = jax.ShapeDtypeStruct(state.shape, f32)
    state, z, edge = call(
        functools.partial(main_kernel, hop),
        [out, buffer(lon, rows, lat), buffer(2, lev, lat)],
        [HBM] + [VMEM] * 5,
        [HBM] + [VMEM] * 2,
        [
            buffer(lon, rows, lat),
            buffer(2, rows + lev, lat),
            buffer(5, lon, lev, lat),
            buffer(lon, rows, lat),
        ],
        [lon, 2],
    )(in_hbm(state), packed, sent, coupling, near_x, far_x)
    z, edge = in_vmem(z), in_vmem(edge)
    for whole, block in ((True, far_p), (False, near_p)):
        state = call(
            functools.partial(finish_kernel, hop, whole),
            out,
            [VMEM] * 3 + [HBM],
            HBM,
            [buffer(rows, lat)],
            [lon],
            {3: 0},
        )(block, z, edge, in_hbm(state))
    return state


def per_device(forcing, trajectory, land_mask, coupling):
    _, mem, var, lev, lon, lat = forcing.shape
    assert lax.axis_size("space") % 2 == 0 and lon >= 2 and STEPS == 2
    state = forcing.reshape(mem * var * lev, lon, lat)
    for hop in range(lax.axis_size("tm") - 1):
        state = advance(hop, state, trajectory[0], land_mask, coupling)
    return state.reshape(forcing.shape)


def solution(mesh):
    return jax.shard_map(
        per_device,
        mesh=mesh,
        in_specs=(
            P("tm", None, None, None, "space", None),
            P("tm", None, None, "space", None),
            P(None, "space", None),
            P(),
        ),
        out_specs=P("tm", None, None, None, "space", None),
        check_vma=False,
    )
```

```python
import functools
import math

import jax
import jax.numpy as jnp
from jax import lax
from jax.experimental import pallas as pl
from jax.experimental.pallas import tpu as pltpu
from jax.sharding import PartitionSpec as P


STEPS = 2
HBM = pl.BlockSpec(memory_space=pltpu.HBM)
VMEM = pl.BlockSpec(memory_space=pltpu.VMEM)


def run_copies(pairs, sem):
    copies = [pltpu.make_async_copy(src, dst, sem.at[i]) for i, (src, dst) in enumerate(pairs)]
    for copy in copies:
        copy.start()
    return copies


def wait_all(copies):
    for copy in copies:
        copy.wait()


def by_parity(body, last):
    even = lax.rem(lax.axis_index("space"), 2) == 0
    pl.when(even)(lambda: body(last, 0))
    pl.when(jnp.logical_not(even))(lambda: body(0, last))


def shifts(x):
    return pltpu.roll(x, x.shape[-1] - 1, 1), pltpu.roll(x, 1, 1)


def stencil(u, v, nu):
    u, v = 0.5 * u, 0.5 * v
    lat = lax.broadcasted_iota(jnp.int32, u.shape, 1)
    north = jnp.where(lat == u.shape[1] - 1, 0.0, nu - v)
    south = jnp.where(lat == 0, 0.0, nu + v)
    return 1.0 - 4.0 * nu, nu - u, nu + u, north, south


def spread(coupling, shape):
    var = coupling.shape[0]
    table = coupling[...]
    return [[jnp.broadcast_to(table[c : c + 1, d : d + 1], shape) for d in range(var)] for c in range(var)]


def mix(pair, block, c):
    width = block[0].shape[1] // pair[c][0].shape[1]
    total = None
    for d, field in enumerate(block):
        term = jnp.tile(pair[c][d], (1, width)) * field
        total = term if total is None else total + term
    return total


class Packed:
    def __init__(self, ref, j, rows, lev):
        self.ref, self.j, self.rows, self.lev = ref, j, rows, lev

    def field(self, base):
        return self.ref[self.j, pl.ds(base, self.lev), :]

    def weights(self):
        u, v, nu = (self.ref[self.j, self.rows + k * self.lev : self.rows + (k + 1) * self.lev, :] for k in range(3))
        return stencil(u, v, nu)


def edges_kernel(hop, x, traj, mask, near, far, wind, open_, sem):
    rows = x.shape[0]
    last = x.shape[1] - 1

    @pl.when(lax.axis_index("tm") == hop)
    def _():
        others = []
        for i, j in enumerate((0, last)):
            others.append((traj.at[0, :, j, :], wind.at[i]))
            others.append((mask.at[:, j, :], open_.at[i]))

        def fill(j_near, j_far):
            fields = [(x.at[:, j, :], ref.at[0:rows, :]) for j, ref in ((j_near, near), (j_far, far))]
            copies = run_copies(others + fields, sem)
            wait_all(copies[: len(others)])
            for j, ref in ((j_near, near), (j_far, far)):
                i = 0 if j == 0 else 1
                nu, half = 0.15 * open_[i].astype(jnp.float32), 0.5 * wind[i]
                ref[rows:, :] = nu + half if j == 0 else nu - half
            wait_all(copies[len(others) :])

        by_parity(fill, last)


def pack_kernel(hop, x, traj, mask, near, far, packed, open_, sem):
    rows, lon = x.shape[0], x.shape[1]
    lev = traj.shape[1]
    last = lon - 1

    @pl.when(lax.axis_index("tm") == hop)
    def _():
        pairs = []
        for j in range(lon):
            pairs.append((mask.at[:, j, :], open_.at[j]))
        for j in range(lon):
            for k in range(2):
                start = rows + k * lev
                pairs.append((traj.at[k, :, j, :], packed.at[j, start : start + lev, :]))
        pairs += [(x.at[:, j, :], packed.at[j, 0:rows, :]) for j in range(1, last)]
        copies = run_copies(pairs, sem)

        def fill(j_near, j_far):
            for j, ref in ((j_near, near), (j_far, far)):
                for r in range(0, rows, lev):
                    packed[j, r : r + lev, :] = ref[r : r + lev, :]

        by_parity(fill, last)
        wait_all(copies[:lon])
        for j in range(lon):
            packed[j, rows + 2 * lev :, :] = 0.15 * open_[j].astype(jnp.float32)
        wait_all(copies[lon:])


def partial_kernel(hop, to_far, packed, coupling, out):
    last = packed.shape[0] - 1
    rows, var = out.shape[0], coupling.shape[0]
    lev = (packed.shape[1] - rows) // 3

    @pl.when(lax.axis_index("tm") == hop)
    def _():
        pair = spread(coupling, (lev, 128))

        def send(j_near, j_far):
            j = j_far if to_far else j_near
            here = Packed(packed, j, rows, lev)
            inner = Packed(packed, 1 if j == 0 else last - 1, rows, lev)
            mid, east, west, north, south = here.weights()
            side = east if j == 0 else west

            def member(m, carry):
                base = pl.multiple_of(m * var * lev, lev)
                block = [here.field(base + d * lev) for d in range(var)]
                for c in range(var):
                    up, low = shifts(block[c])
                    total = mid * block[c] + side * inner.field(base + c * lev)
                    total += north * up + south * low
                    out[pl.ds(base + c * lev, lev), :] = total + mix(pair, block, c)
                return carry

            lax.fori_loop(0, rows // (var * lev), member, 0)

        by_parity(send, last)


def step(coef, coupling, j, centre, east, west):
    block = [centre(d) for d in range(len(coupling))]
    for c, field in enumerate(block):
        up, low = shifts(field)
        total = coef[0, j] * field + coef[3, j] * up + coef[4, j] * low
        if east is not None:
            total += coef[1, j] * east(c)
        if west is not None:
            total += coef[2, j] * west(c)
        yield c, total + mix(coupling, block, c)


def reader(ref, base, lev, *index):
    return lambda d: ref[(*index, pl.ds(base + d * lev, lev), slice(None))]


def main_kernel(hop, own, sent, coupling, z, coef, ss, sem):
    rows, lon = own.shape[0], own.shape[1]
    var = coupling.shape[0]
    lev = (sent.shape[1] - rows) // 3
    members = rows // (var * lev)

    @pl.when(lax.axis_index("tm") == hop + 1)
    def _():
        forces = run_copies([(own.at[:, j, :], z.at[j]) for j in range(lon)], sem)
        for j in range(lon):
            for k, value in enumerate(Packed(sent, j, rows, lev).weights()):
                coef[k, j] = value
        pair = spread(coupling, (lev, 128))

        def steps(ref, base):
            fields = {j: reader(ref, base, lev, j) for j in range(lon)}
            for j in range(lon):
                for c, total in step(coef, pair, j, fields[j], fields.get(j + 1), fields.get(j - 1)):
                    yield j, pl.ds(base + c * lev, lev), total

        def first(m, carry):
            for j, at, total in steps(sent, pl.multiple_of(m * var * lev, lev)):
                ss[j, at, :] = total
            return carry

        def second(m, carry):
            for j, at, total in steps(ss, pl.multiple_of(m * var * lev, lev)):
                z[j, at, :] += total
            return carry

        lax.fori_loop(0, members, first, 0)
        wait_all(forces)
        lax.fori_loop(0, members, second, 0)


def sides_kernel(hop, own, packed, sent, coupling, near, far, z, coef, out, ze, inner, sem):
    rows, lon = own.shape[0], own.shape[1]
    var = coupling.shape[0]
    lev = coef.shape[2]
    last = lon - 1
    members = rows // (var * lev)
    row = lax.axis_index("tm")

    @pl.when(row == hop)
    def _():
        wait_all(run_copies([(packed.at[j, 0:rows, :], out.at[:, j, :]) for j in range(lon)], sem))

    @pl.when(jnp.logical_and(row != hop, row != hop + 1))
    def _():
        for j in range(lon):
            wait_all(run_copies([(own.at[:, j, :], inner.at[0])], sem))
            wait_all(run_copies([(inner.at[0], out.at[:, j, :])], sem))

    @pl.when(row == hop + 1)
    def _():
        pair = spread(coupling, (lev, 128))

        def body(j_near, j_far):
            edges = {j_near: near, j_far: far}

            def added(j, base):
                weight = coef[2 if j == 0 else 1, j]
                return lambda d: weight * edges[j][pl.ds(base + d * lev, lev), :]

            def between(m, carry):
                base = pl.multiple_of(m * var * lev, lev)
                for j in range(1, last):
                    for c in range(var):
                        at = pl.ds(base + c * lev, lev)
                        total = z[j, at, :]
                        if j == 1:
                            total += coef[2, j] * added(0, base)(c)
                        if j == last - 1:
                            total += coef[1, j] * added(last, base)(c)
                        inner[j - 1, at, :] = total
                return carry

            lax.fori_loop(0, members, between, 0)
            copies = run_copies([(inner.at[j - 1], out.at[:, j, :]) for j in range(1, last)], sem)

            def outermost(m, carry):
                base = pl.multiple_of(m * var * lev, lev)
                for i, j in enumerate((0, last)):
                    weight = coef[2 if j == 0 else 1, j] * edges[j][rows:, :]
                    for c, total in step(coef, pair, j, added(j, base), None, None):
                        at = pl.ds(base + c * lev, lev)
                        ze[i, at, :] = z[j, at, :] + total + weight * sent[j, at, :]
                return carry

            lax.fori_loop(0, members, outermost, 0)
            wait_all(copies)

        by_parity(body, last)


def finish_kernel(hop, parts, near, far, ze, coef, out_in, out, done, sem):
    del out_in
    rows = ze.shape[1]
    lon, lev = coef.shape[1:3]

    @pl.when(lax.axis_index("tm") == hop + 1)
    def _():
        def body(j_near, j_far):
            copies = []
            for j, block in ((j_far, far), (j_near, near)):
                i = 0 if j == 0 else 1
                weight = coef[2 if j == 0 else 1, j]
                for part in range(parts):
                    lo, hi = rows * part // parts, rows * (part + 1) // parts
                    for r in range(lo, hi, lev):
                        done[i, r : r + lev, :] = ze[i, r : r + lev, :] + weight * block[r : r + lev, :]
                    copy = pltpu.make_async_copy(
                        done.at[i, lo:hi, :], out.at[lo:hi, j, :], sem.at[i * parts + part]
                    )
                    copy.start()
                    copies.append(copy)
            wait_all(copies)

        by_parity(body, lon - 1)


def call(kernel, out_shape, in_specs, out_specs, scratch, semaphores, aliases=None):
    room = sum(4 * math.prod(ref.inner_aval.shape) for ref in scratch)
    return pl.pallas_call(
        kernel,
        out_shape=out_shape,
        in_specs=in_specs,
        out_specs=out_specs,
        scratch_shapes=scratch + [pltpu.SemaphoreType.DMA((count,)) for count in semaphores],
        compiler_params=pltpu.CompilerParams(vmem_limit_bytes=room + 2**22),
        input_output_aliases=aliases or {},
    )


def advance(hop, state, traj, land_mask, coupling):
    rows, lon, lat = state.shape
    lev = traj.shape[1]
    n = lax.axis_size("space")
    f32 = jnp.float32

    def buffer(*dims, dtype=f32):
        return pltpu.VMEM(dims, dtype)

    def in_vmem(array):
        return pltpu.with_memory_space_constraint(array, pltpu.VMEM)

    def in_hbm(array):
        return pltpu.with_memory_space_constraint(array, pltpu.HBM)

    def moved(block, move):
        pairs = [(hop * n + s, (hop + 1) * n + move(s) % n) for s in range(n)]
        pairs += [((hop + 1) * n + s, hop * n + s) for s in range(n)]
        pairs += [(r, r) for r in range(lax.axis_size("tm") * n) if r // n not in (hop, hop + 1)]
        block = lax.ppermute(block, ("tm", "space"), pairs)
        return in_vmem(block)

    def to_near(s):
        return s + 1 if s % 2 == 0 else s - 1

    def to_far(s):
        return s - 1 if s % 2 == 0 else s + 1

    coupling = in_vmem(coupling)
    held = in_hbm(state), in_hbm(traj), in_hbm(land_mask)
    near, far = call(
        functools.partial(edges_kernel, hop),
        [buffer(rows + lev, lat)] * 2,
        [HBM] * 3,
        [VMEM] * 2,
        [buffer(2, lev, lat), buffer(2, lev, lat, dtype=jnp.int32)],
        [6],
    )(*held)
    near_x = moved(near, to_near)
    far_x = moved(far, to_far)
    packed = call(
        functools.partial(pack_kernel, hop),
        buffer(lon, rows + 3 * lev, lat),
        [HBM] * 3 + [VMEM] * 2,
        VMEM,
        [buffer(lon, lev, lat, dtype=jnp.int32)],
        [4 * lon - 2],
    )(*held, in_vmem(near), in_vmem(far))
    sent = moved(packed, lambda s: s)
    packed = in_vmem(packed)
    packed = in_vmem(packed)

    def partial(side):
        return call(
            functools.partial(partial_kernel, hop, side == "far"),
            buffer(rows, lat),
            [VMEM] * 2,
            VMEM,
            [],
            [],
        )(packed, coupling)

    far_p = moved(partial("far"), to_far)
    near_p = moved(partial("near"), to_near)
    z, coef = call(
        functools.partial(main_kernel, hop),
        [buffer(lon, rows, lat), buffer(5, lon, lev, lat)],
        [HBM] + [VMEM] * 2,
        [VMEM] * 2,
        [buffer(lon, rows, lat)],
        [lon],
    )(held[0], sent, coupling)
    z, coef = in_vmem(z), in_vmem(coef)
    out = jax.ShapeDtypeStruct(state.shape, f32)
    state, ze = call(
        functools.partial(sides_kernel, hop),
        [out, buffer(2, rows, lat)],
        [HBM] + [VMEM] * 7,
        [HBM, VMEM],
        [buffer(lon - 2, rows, lat)],
        [lon],
    )(held[0], packed, sent, coupling, near_x, far_x, z, coef)
    parts = 2
    state = call(
        functools.partial(finish_kernel, hop, parts),
        out,
        [VMEM] * 4 + [HBM],
        HBM,
        [buffer(2, rows, lat)],
        [2 * parts],
        {4: 0},
    )(near_p, far_p, in_vmem(ze), coef, in_hbm(state))
    return state


def per_device(forcing, trajectory, land_mask, coupling):
    _, mem, var, lev, lon, lat = forcing.shape
    assert lax.axis_size("space") % 2 == 0 and lon >= 3 and STEPS == 2
    state = forcing.reshape(mem * var * lev, lon, lat)
    for hop in range(lax.axis_size("tm") - 1):
        state = advance(hop, state, trajectory[0], land_mask, coupling)
    return state.reshape(forcing.shape)


def solution(mesh):
    return jax.shard_map(
        per_device,
        mesh=mesh,
        in_specs=(
            P("tm", None, None, None, "space", None),
            P("tm", None, None, "space", None),
            P(None, "space", None),
            P(),
        ),
        out_specs=P("tm", None, None, None, "space", None),
        check_vma=False,
    )
```

```python
import functools
import math

import jax
import jax.numpy as jnp
from jax import lax
from jax.experimental import pallas as pl
from jax.experimental.pallas import tpu as pltpu
from jax.sharding import PartitionSpec as P


STEPS = 2
HBM = pl.BlockSpec(memory_space=pltpu.HBM)
VMEM = pl.BlockSpec(memory_space=pltpu.VMEM)


def run_copies(pairs, sem):
    copies = [pltpu.make_async_copy(src, dst, sem.at[i]) for i, (src, dst) in enumerate(pairs)]
    for copy in copies:
        copy.start()
    return copies


def wait_all(copies):
    for copy in copies:
        copy.wait()


def by_parity(body, last):
    even = lax.rem(lax.axis_index("space"), 2) == 0
    pl.when(even)(lambda: body(last, 0))
    pl.when(jnp.logical_not(even))(lambda: body(0, last))


def shifts(x):
    return pltpu.roll(x, x.shape[-1] - 1, 1), pltpu.roll(x, 1, 1)


def stencil(u, v, nu):
    u, v = 0.5 * u, 0.5 * v
    lat = lax.broadcasted_iota(jnp.int32, u.shape, 1)
    north = jnp.where(lat == u.shape[1] - 1, 0.0, nu - v)
    south = jnp.where(lat == 0, 0.0, nu + v)
    return 1.0 - 4.0 * nu, nu - u, nu + u, north, south


def spread(coupling, shape):
    var = coupling.shape[0]
    table = coupling[...]
    return [[jnp.broadcast_to(table[c : c + 1, d : d + 1], shape) for d in range(var)] for c in range(var)]


def mix(pair, block, c):
    width = block[0].shape[1] // pair[c][0].shape[1]
    total = None
    for d, field in enumerate(block):
        term = jnp.tile(pair[c][d], (1, width)) * field
        total = term if total is None else total + term
    return total


class Packed:
    def __init__(self, ref, j, rows, lev):
        self.ref, self.j, self.rows, self.lev = ref, j, rows, lev

    def field(self, base):
        return self.ref[self.j, pl.ds(base, self.lev), :]

    def weights(self):
        u, v, nu = (self.ref[self.j, self.rows + k * self.lev : self.rows + (k + 1) * self.lev, :] for k in range(3))
        return stencil(u, v, nu)


def entry_weight(j, u, mask):
    nu, half = 0.15 * mask.astype(jnp.float32), 0.5 * u
    return nu + half if j == 0 else nu - half


def edge_kernel(hop, x, traj, mask, near, wind, open_, sem):
    rows = x.shape[0]

    @pl.when(lax.axis_index("tm") == hop)
    def _():
        def fill(j_near, j_far):
            pairs = [
                (x.at[:, j_near, :], near.at[0:rows, :]),
                (traj.at[0, :, j_near, :], wind),
                (mask.at[:, j_near, :], open_),
            ]
            copies = run_copies(pairs, sem)
            wait_all(copies[1:])
            near[rows:, :] = entry_weight(j_near, wind[...], open_[...])
            wait_all(copies[:1])

        by_parity(fill, x.shape[1] - 1)


def pack_kernel(hop, x, traj, mask, near, packed, far, open_, sem):
    rows, lon = x.shape[0], x.shape[1]
    lev = traj.shape[1]
    last = lon - 1

    @pl.when(lax.axis_index("tm") == hop)
    def _():
        def fill(j_near, j_far):
            masks = [(mask.at[:, j, :], open_.at[j]) for j in range(lon)]
            wind = []
            for j in range(lon):
                for k in range(2):
                    start = rows + k * lev
                    wind.append((traj.at[k, :, j, :], packed.at[j, start : start + lev, :]))
            others = [j_far] + [j for j in range(1, last)]
            fields = [(x.at[:, j, :], packed.at[j, 0:rows, :]) for j in others]
            copies = run_copies(masks + wind + fields, sem)
            for r in range(0, rows, lev):
                packed[j_near, r : r + lev, :] = near[r : r + lev, :]
            small = len(masks) + len(wind)
            wait_all(copies[:small])
            for j in range(lon):
                packed[j, rows + 2 * lev :, :] = 0.15 * open_[j].astype(jnp.float32)
            far[rows:, :] = entry_weight(j_far, packed[j_far, rows : rows + lev, :], open_[j_far])
            wait_all(copies[small : small + 1])
            for r in range(0, rows, lev):
                far[r : r + lev, :] = packed[j_far, r : r + lev, :]
            wait_all(copies[small + 1 :])

        by_parity(fill, last)


def partial_kernel(hop, to_far, packed, coupling, out):
    last = packed.shape[0] - 1
    rows, var = out.shape[0], coupling.shape[0]
    lev = (packed.shape[1] - rows) // 3

    @pl.when(lax.axis_index("tm") == hop)
    def _():
        pair = spread(coupling, (lev, 128))

        def send(j_near, j_far):
            j = j_far if to_far else j_near
            here = Packed(packed, j, rows, lev)
            inner = Packed(packed, 1 if j == 0 else last - 1, rows, lev)
            mid, east, west, north, south = here.weights()
            side = east if j == 0 else west

            def member(m, carry):
                base = pl.multiple_of(m * var * lev, lev)
                block = [here.field(base + d * lev) for d in range(var)]
                for c in range(var):
                    up, low = shifts(block[c])
                    total = mid * block[c] + side * inner.field(base + c * lev)
                    total += north * up + south * low
                    out[pl.ds(base + c * lev, lev), :] = total + mix(pair, block, c)
                return carry

            lax.fori_loop(0, rows // (var * lev), member, 0)

        by_parity(send, last)


def step(coef, coupling, j, centre, east, west):
    block = [centre(d) for d in range(len(coupling))]
    for c, field in enumerate(block):
        up, low = shifts(field)
        total = coef[0, j] * field + coef[3, j] * up + coef[4, j] * low
        if east is not None:
            total += coef[1, j] * east(c)
        if west is not None:
            total += coef[2, j] * west(c)
        yield c, total + mix(coupling, block, c)


def reader(ref, base, lev, *index):
    return lambda d: ref[(*index, pl.ds(base + d * lev, lev), slice(None))]


def main_kernel(hop, own, sent, coupling, z, coef, ss, sem):
    rows, lon = own.shape[0], own.shape[1]
    var = coupling.shape[0]
    lev = (sent.shape[1] - rows) // 3
    members = rows // (var * lev)

    @pl.when(lax.axis_index("tm") == hop + 1)
    def _():
        forces = run_copies([(own.at[:, j, :], z.at[j]) for j in range(lon)], sem)
        for j in range(lon):
            for k, value in enumerate(Packed(sent, j, rows, lev).weights()):
                coef[k, j] = value
        pair = spread(coupling, (lev, 128))

        def steps(ref, base):
            fields = {j: reader(ref, base, lev, j) for j in range(lon)}
            for j in range(lon):
                for c, total in step(coef, pair, j, fields[j], fields.get(j + 1), fields.get(j - 1)):
                    yield j, pl.ds(base + c * lev, lev), total

        def first(m, carry):
            for j, at, total in steps(sent, pl.multiple_of(m * var * lev, lev)):
                ss[j, at, :] = total
            return carry

        def second(m, carry):
            for j, at, total in steps(ss, pl.multiple_of(m * var * lev, lev)):
                z[j, at, :] += total
            return carry

        lax.fori_loop(0, members, first, 0)
        wait_all(forces)
        lax.fori_loop(0, members, second, 0)


def sides_kernel(hop, own, packed, sent, coupling, near, far, z, coef, out, ze, inner, sem):
    rows, lon = own.shape[0], own.shape[1]
    var = coupling.shape[0]
    lev = coef.shape[2]
    last = lon - 1
    members = rows // (var * lev)
    row = lax.axis_index("tm")

    @pl.when(row == hop)
    def _():
        wait_all(run_copies([(packed.at[j, 0:rows, :], out.at[:, j, :]) for j in range(lon)], sem))

    @pl.when(jnp.logical_and(row != hop, row != hop + 1))
    def _():
        for j in range(lon):
            wait_all(run_copies([(own.at[:, j, :], inner.at[0])], sem))
            wait_all(run_copies([(inner.at[0], out.at[:, j, :])], sem))

    @pl.when(row == hop + 1)
    def _():
        pair = spread(coupling, (lev, 128))

        def body(j_near, j_far):
            edges = {j_near: near, j_far: far}

            def added(j, base):
                weight = coef[2 if j == 0 else 1, j]
                return lambda d: weight * edges[j][pl.ds(base + d * lev, lev), :]

            def between(m, carry):
                base = pl.multiple_of(m * var * lev, lev)
                for j in range(1, last):
                    for c in range(var):
                        at = pl.ds(base + c * lev, lev)
                        total = z[j, at, :]
                        if j == 1:
                            total += coef[2, j] * added(0, base)(c)
                        if j == last - 1:
                            total += coef[1, j] * added(last, base)(c)
                        inner[j - 1, at, :] = total
                return carry

            lax.fori_loop(0, members, between, 0)
            copies = run_copies([(inner.at[j - 1], out.at[:, j, :]) for j in range(1, last)], sem)

            def outermost(m, carry):
                base = pl.multiple_of(m * var * lev, lev)
                for i, j in enumerate((0, last)):
                    weight = coef[2 if j == 0 else 1, j] * edges[j][rows:, :]
                    for c, total in step(coef, pair, j, added(j, base), None, None):
                        at = pl.ds(base + c * lev, lev)
                        ze[i, at, :] = z[j, at, :] + total + weight * sent[j, at, :]
                return carry

            lax.fori_loop(0, members, outermost, 0)
            wait_all(copies)

        by_parity(body, last)


def finish_kernel(hop, parts, near, far, ze, coef, out_in, out, done, sem):
    del out_in
    rows = ze.shape[1]
    lon, lev = coef.shape[1:3]

    @pl.when(lax.axis_index("tm") == hop + 1)
    def _():
        def body(j_near, j_far):
            copies = []
            for j, block in ((j_far, far), (j_near, near)):
                i = 0 if j == 0 else 1
                weight = coef[2 if j == 0 else 1, j]
                for part in range(parts):
                    lo, hi = rows * part // parts, rows * (part + 1) // parts
                    for r in range(lo, hi, lev):
                        done[i, r : r + lev, :] = ze[i, r : r + lev, :] + weight * block[r : r + lev, :]
                    copy = pltpu.make_async_copy(
                        done.at[i, lo:hi, :], out.at[lo:hi, j, :], sem.at[i * parts + part]
                    )
                    copy.start()
                    copies.append(copy)
            wait_all(copies)

        by_parity(body, lon - 1)


def call(kernel, out_shape, in_specs, out_specs, scratch, semaphores, aliases=None):
    room = sum(4 * math.prod(ref.inner_aval.shape) for ref in scratch)
    return pl.pallas_call(
        kernel,
        out_shape=out_shape,
        in_specs=in_specs,
        out_specs=out_specs,
        scratch_shapes=scratch + [pltpu.SemaphoreType.DMA((count,)) for count in semaphores],
        compiler_params=pltpu.CompilerParams(vmem_limit_bytes=room + 2**22),
        input_output_aliases=aliases or {},
    )


def advance(hop, state, traj, land_mask, coupling):
    rows, lon, lat = state.shape
    lev = traj.shape[1]
    n = lax.axis_size("space")
    f32 = jnp.float32

    def buffer(*dims, dtype=f32):
        return pltpu.VMEM(dims, dtype)

    def in_vmem(array):
        return pltpu.with_memory_space_constraint(array, pltpu.VMEM)

    def in_hbm(array):
        return pltpu.with_memory_space_constraint(array, pltpu.HBM)

    def moved(block, move):
        pairs = [(hop * n + s, (hop + 1) * n + move(s) % n) for s in range(n)]
        pairs += [((hop + 1) * n + s, hop * n + s) for s in range(n)]
        pairs += [(r, r) for r in range(lax.axis_size("tm") * n) if r // n not in (hop, hop + 1)]
        block = lax.ppermute(block, ("tm", "space"), pairs)
        return in_vmem(block)

    def to_near(s):
        return s + 1 if s % 2 == 0 else s - 1

    def to_far(s):
        return s - 1 if s % 2 == 0 else s + 1

    coupling = in_vmem(coupling)
    held = in_hbm(state), in_hbm(traj), in_hbm(land_mask)
    near = call(
        functools.partial(edge_kernel, hop),
        buffer(rows + lev, lat),
        [HBM] * 3,
        VMEM,
        [buffer(lev, lat), buffer(lev, lat, dtype=jnp.int32)],
        [3],
    )(*held)
    near_x = moved(near, to_near)
    packed, far = call(
        functools.partial(pack_kernel, hop),
        [buffer(lon, rows + 3 * lev, lat), buffer(rows + lev, lat)],
        [HBM] * 3 + [VMEM],
        [VMEM] * 2,
        [buffer(lon, lev, lat, dtype=jnp.int32)],
        [4 * lon - 1],
    )(*held, in_vmem(near))
    far_x = moved(far, to_far)
    sent = moved(packed, lambda s: s)
    packed = in_vmem(packed)
    packed = in_vmem(packed)

    def partial(side):
        return call(
            functools.partial(partial_kernel, hop, side == "far"),
            buffer(rows, lat),
            [VMEM] * 2,
            VMEM,
            [],
            [],
        )(packed, coupling)

    far_p = moved(partial("far"), to_far)
    near_p = moved(partial("near"), to_near)
    z, coef = call(
        functools.partial(main_kernel, hop),
        [buffer(lon, rows, lat), buffer(5, lon, lev, lat)],
        [HBM] + [VMEM] * 2,
        [VMEM] * 2,
        [buffer(lon, rows, lat)],
        [lon],
    )(held[0], sent, coupling)
    z, coef = in_vmem(z), in_vmem(coef)
    out = jax.ShapeDtypeStruct(state.shape, f32)
    state, ze = call(
        functools.partial(sides_kernel, hop),
        [out, buffer(2, rows, lat)],
        [HBM] + [VMEM] * 7,
        [HBM, VMEM],
        [buffer(lon - 2, rows, lat)],
        [lon],
    )(held[0], packed, sent, coupling, near_x, far_x, z, coef)
    parts = 2
    state = call(
        functools.partial(finish_kernel, hop, parts),
        out,
        [VMEM] * 4 + [HBM],
        HBM,
        [buffer(2, rows, lat)],
        [2 * parts],
        {4: 0},
    )(near_p, far_p, in_vmem(ze), coef, in_hbm(state))
    return state


def per_device(forcing, trajectory, land_mask, coupling):
    _, mem, var, lev, lon, lat = forcing.shape
    assert lax.axis_size("space") % 2 == 0 and lon >= 3 and STEPS == 2
    state = forcing.reshape(mem * var * lev, lon, lat)
    for hop in range(lax.axis_size("tm") - 1):
        state = advance(hop, state, trajectory[0], land_mask, coupling)
    return state.reshape(forcing.shape)


def solution(mesh):
    return jax.shard_map(
        per_device,
        mesh=mesh,
        in_specs=(
            P("tm", None, None, None, "space", None),
            P("tm", None, None, "space", None),
            P(None, "space", None),
            P(),
        ),
        out_specs=P("tm", None, None, None, "space", None),
        check_vma=False,
    )
```

```python
import functools
import math

import jax
import jax.numpy as jnp
from jax import lax
from jax.experimental import pallas as pl
from jax.experimental.pallas import tpu as pltpu
from jax.sharding import PartitionSpec as P


STEPS = 2
HBM = pl.BlockSpec(memory_space=pltpu.HBM)
VMEM = pl.BlockSpec(memory_space=pltpu.VMEM)


def run_copies(pairs, sem):
    copies = [pltpu.make_async_copy(src, dst, sem.at[i]) for i, (src, dst) in enumerate(pairs)]
    for copy in copies:
        copy.start()
    return copies


def wait_all(copies):
    for copy in copies:
        copy.wait()


def by_parity(body, last):
    even = lax.rem(lax.axis_index("space"), 2) == 0
    pl.when(even)(lambda: body(last, 0))
    pl.when(jnp.logical_not(even))(lambda: body(0, last))


def shifts(x):
    return pltpu.roll(x, x.shape[-1] - 1, 1), pltpu.roll(x, 1, 1)


def stencil(u, v, nu):
    u, v = 0.5 * u, 0.5 * v
    lat = lax.broadcasted_iota(jnp.int32, u.shape, 1)
    north = jnp.where(lat == u.shape[1] - 1, 0.0, nu - v)
    south = jnp.where(lat == 0, 0.0, nu + v)
    return 1.0 - 4.0 * nu, nu - u, nu + u, north, south


def spread(coupling, shape):
    var = coupling.shape[0]
    table = coupling[...]
    return [[jnp.broadcast_to(table[c : c + 1, d : d + 1], shape) for d in range(var)] for c in range(var)]


def mix(pair, block, c):
    width = block[0].shape[1] // pair[c][0].shape[1]
    total = None
    for d, field in enumerate(block):
        term = jnp.tile(pair[c][d], (1, width)) * field
        total = term if total is None else total + term
    return total


class Packed:
    def __init__(self, ref, j, rows, lev):
        self.ref, self.j, self.rows, self.lev = ref, j, rows, lev

    def field(self, base):
        return self.ref[self.j, pl.ds(base, self.lev), :]

    def weights(self):
        u, v, nu = (self.ref[self.j, self.rows + k * self.lev : self.rows + (k + 1) * self.lev, :] for k in range(3))
        return stencil(u, v, nu)


def entry_weight(j, u, mask):
    nu, half = 0.15 * mask.astype(jnp.float32), 0.5 * u
    return nu + half if j == 0 else nu - half


def edge_kernel(hop, x, traj, mask, near, wind, open_, sem):
    rows = x.shape[0]

    @pl.when(lax.axis_index("tm") == hop)
    def _():
        def fill(j_near, j_far):
            pairs = [
                (x.at[:, j_near, :], near.at[0:rows, :]),
                (traj.at[0, :, j_near, :], wind),
                (mask.at[:, j_near, :], open_),
            ]
            copies = run_copies(pairs, sem)
            wait_all(copies[1:])
            near[rows:, :] = entry_weight(j_near, wind[...], open_[...])
            wait_all(copies[:1])

        by_parity(fill, x.shape[1] - 1)


def pack_kernel(hop, x, traj, mask, near, packed, far, open_, sem):
    rows, lon = x.shape[0], x.shape[1]
    lev = traj.shape[1]
    last = lon - 1

    @pl.when(lax.axis_index("tm") == hop)
    def _():
        def fill(j_near, j_far):
            masks = [(mask.at[:, j, :], open_.at[j]) for j in range(lon)]
            wind = []
            for j in range(lon):
                for k in range(2):
                    start = rows + k * lev
                    wind.append((traj.at[k, :, j, :], packed.at[j, start : start + lev, :]))
            others = [j_far] + [j for j in range(1, last)]
            fields = [(x.at[:, j, :], packed.at[j, 0:rows, :]) for j in others]
            copies = run_copies(masks + wind + fields, sem)
            for r in range(0, rows, lev):
                packed[j_near, r : r + lev, :] = near[r : r + lev, :]
            small = len(masks) + len(wind)
            wait_all(copies[:small])
            for j in range(lon):
                packed[j, rows + 2 * lev :, :] = 0.15 * open_[j].astype(jnp.float32)
            far[rows:, :] = entry_weight(j_far, packed[j_far, rows : rows + lev, :], open_[j_far])
            wait_all(copies[small : small + 1])
            for r in range(0, rows, lev):
                far[r : r + lev, :] = packed[j_far, r : r + lev, :]
            wait_all(copies[small + 1 :])

        by_parity(fill, last)


def partial_kernel(hop, to_far, packed, coupling, *outs):
    last = packed.shape[0] - 1
    var = coupling.shape[0]
    rows = sum(out.shape[0] for out in outs)
    lev = (packed.shape[1] - rows) // 3

    @pl.when(lax.axis_index("tm") == hop)
    def _():
        pair = spread(coupling, (lev, 128))

        def send(j_near, j_far):
            j = j_far if to_far else j_near
            here = Packed(packed, j, rows, lev)
            inner = Packed(packed, 1 if j == 0 else last - 1, rows, lev)
            mid, east, west, north, south = here.weights()
            side = east if j == 0 else west
            lo = 0
            for out in outs:

                def member(m, carry, lo=lo, out=out):
                    base = pl.multiple_of(m * var * lev, lev)
                    block = [here.field(lo + base + d * lev) for d in range(var)]
                    for c in range(var):
                        up, low = shifts(block[c])
                        total = mid * block[c] + side * inner.field(lo + base + c * lev)
                        total += north * up + south * low
                        out[pl.ds(base + c * lev, lev), :] = total + mix(pair, block, c)
                    return carry

                lax.fori_loop(0, out.shape[0] // (var * lev), member, 0, unroll=True)
                lo += out.shape[0]

        by_parity(send, last)


def step(coef, coupling, j, centre, east, west):
    block = [centre(d) for d in range(len(coupling))]
    for c, field in enumerate(block):
        up, low = shifts(field)
        total = coef[0, j] * field + coef[3, j] * up + coef[4, j] * low
        if east is not None:
            total += coef[1, j] * east(c)
        if west is not None:
            total += coef[2, j] * west(c)
        yield c, total + mix(coupling, block, c)


def reader(ref, base, lev, *index):
    return lambda d: ref[(*index, pl.ds(base + d * lev, lev), slice(None))]


def main_kernel(hop, own, sent, coupling, z, coef, ss, sem):
    rows, lon = own.shape[0], own.shape[1]
    var = coupling.shape[0]
    lev = (sent.shape[1] - rows) // 3
    members = rows // (var * lev)

    @pl.when(lax.axis_index("tm") == hop + 1)
    def _():
        forces = run_copies([(own.at[:, j, :], z.at[j]) for j in range(lon)], sem)
        for j in range(lon):
            for k, value in enumerate(Packed(sent, j, rows, lev).weights()):
                coef[k, j] = value
        pair = spread(coupling, (lev, 128))

        def steps(ref, base):
            fields = {j: reader(ref, base, lev, j) for j in range(lon)}
            for j in range(lon):
                for c, total in step(coef, pair, j, fields[j], fields.get(j + 1), fields.get(j - 1)):
                    yield j, pl.ds(base + c * lev, lev), total

        def first(m, carry):
            for j, at, total in steps(sent, pl.multiple_of(m * var * lev, lev)):
                ss[j, at, :] = total
            return carry

        def second(m, carry):
            for j, at, total in steps(ss, pl.multiple_of(m * var * lev, lev)):
                z[j, at, :] += total
            return carry

        lax.fori_loop(0, members, first, 0)
        wait_all(forces)
        lax.fori_loop(0, members, second, 0)


def sides_kernel(hop, own, packed, sent, coupling, near, far, z, coef, out, ze, inner, sem):
    rows, lon = own.shape[0], own.shape[1]
    var = coupling.shape[0]
    lev = coef.shape[2]
    last = lon - 1
    members = rows // (var * lev)
    row = lax.axis_index("tm")

    @pl.when(row == hop)
    def _():
        wait_all(run_copies([(packed.at[j, 0:rows, :], out.at[:, j, :]) for j in range(lon)], sem))

    @pl.when(jnp.logical_and(row != hop, row != hop + 1))
    def _():
        for j in range(lon):
            wait_all(run_copies([(own.at[:, j, :], inner.at[0])], sem))
            wait_all(run_copies([(inner.at[0], out.at[:, j, :])], sem))

    @pl.when(row == hop + 1)
    def _():
        pair = spread(coupling, (lev, 128))

        def body(j_near, j_far):
            edges = {j_near: near, j_far: far}

            def added(j, base):
                weight = coef[2 if j == 0 else 1, j]
                return lambda d: weight * edges[j][pl.ds(base + d * lev, lev), :]

            def between(m, carry):
                base = pl.multiple_of(m * var * lev, lev)
                for j in range(1, last):
                    for c in range(var):
                        at = pl.ds(base + c * lev, lev)
                        total = z[j, at, :]
                        if j == 1:
                            total += coef[2, j] * added(0, base)(c)
                        if j == last - 1:
                            total += coef[1, j] * added(last, base)(c)
                        inner[j - 1, at, :] = total
                return carry

            lax.fori_loop(0, members, between, 0)
            copies = run_copies([(inner.at[j - 1], out.at[:, j, :]) for j in range(1, last)], sem)

            def outermost(m, carry):
                base = pl.multiple_of(m * var * lev, lev)
                for i, j in enumerate((0, last)):
                    weight = coef[2 if j == 0 else 1, j] * edges[j][rows:, :]
                    for c, total in step(coef, pair, j, added(j, base), None, None):
                        at = pl.ds(base + c * lev, lev)
                        ze[i, at, :] = z[j, at, :] + total + weight * sent[j, at, :]
                return carry

            lax.fori_loop(0, members, outermost, 0)
            wait_all(copies)

        by_parity(body, last)


def finish_kernel(hop, lo, near, far, ze, coef, out_in, out, done, sem):
    del out_in
    rows = near.shape[0]
    lon, lev = coef.shape[1:3]

    @pl.when(lax.axis_index("tm") == hop + 1)
    def _():
        def body(j_near, j_far):
            copies = []
            for j, block in ((j_far, far), (j_near, near)):
                i = 0 if j == 0 else 1
                weight = coef[2 if j == 0 else 1, j]
                for r in range(0, rows, lev):
                    done[i, r : r + lev, :] = ze[i, lo + r : lo + r + lev, :] + weight * block[r : r + lev, :]
                copies.append(pltpu.make_async_copy(done.at[i], out.at[lo : lo + rows, j, :], sem.at[i]))
                copies[-1].start()
            wait_all(copies)

        by_parity(body, lon - 1)


def call(kernel, out_shape, in_specs, out_specs, scratch, semaphores, aliases=None):
    room = sum(4 * math.prod(ref.inner_aval.shape) for ref in scratch)
    return pl.pallas_call(
        kernel,
        out_shape=out_shape,
        in_specs=in_specs,
        out_specs=out_specs,
        scratch_shapes=scratch + [pltpu.SemaphoreType.DMA((count,)) for count in semaphores],
        compiler_params=pltpu.CompilerParams(vmem_limit_bytes=room + 2**22),
        input_output_aliases=aliases or {},
    )


def advance(hop, state, traj, land_mask, coupling):
    rows, lon, lat = state.shape
    var, lev = coupling.shape[0], traj.shape[1]
    n = lax.axis_size("space")
    f32 = jnp.float32

    def buffer(*dims, dtype=f32):
        return pltpu.VMEM(dims, dtype)

    def in_vmem(array):
        return pltpu.with_memory_space_constraint(array, pltpu.VMEM)

    def in_hbm(array):
        return pltpu.with_memory_space_constraint(array, pltpu.HBM)

    def moved(block, move):
        pairs = [(hop * n + s, (hop + 1) * n + move(s) % n) for s in range(n)]
        pairs += [((hop + 1) * n + s, hop * n + s) for s in range(n)]
        pairs += [(r, r) for r in range(lax.axis_size("tm") * n) if r // n not in (hop, hop + 1)]
        block = lax.ppermute(block, ("tm", "space"), pairs)
        return in_vmem(block)

    def to_near(s):
        return s + 1 if s % 2 == 0 else s - 1

    def to_far(s):
        return s - 1 if s % 2 == 0 else s + 1

    coupling = in_vmem(coupling)
    held = in_hbm(state), in_hbm(traj), in_hbm(land_mask)
    near = call(
        functools.partial(edge_kernel, hop),
        buffer(rows + lev, lat),
        [HBM] * 3,
        VMEM,
        [buffer(lev, lat), buffer(lev, lat, dtype=jnp.int32)],
        [3],
    )(*held)
    near_x = moved(near, to_near)
    packed, far = call(
        functools.partial(pack_kernel, hop),
        [buffer(lon, rows + 3 * lev, lat), buffer(rows + lev, lat)],
        [HBM] * 3 + [VMEM],
        [VMEM] * 2,
        [buffer(lon, lev, lat, dtype=jnp.int32)],
        [4 * lon - 1],
    )(*held, in_vmem(near))
    far_x = moved(far, to_far)
    sent = moved(packed, lambda s: s)
    packed = in_vmem(packed)
    packed = in_vmem(packed)

    members = rows // (var * lev)
    first = members - members // 4
    sizes = [size * var * lev for size in (first, members - first) if size]

    def partial(side, move):
        outs = call(
            functools.partial(partial_kernel, hop, side == "far"),
            [buffer(size, lat) for size in sizes],
            [VMEM] * 2,
            [VMEM] * len(sizes),
            [],
            [],
        )(packed, coupling)
        return [moved(block, move) for block in outs]

    near_p = partial("near", to_near)
    far_p = partial("far", to_far)
    z, coef = call(
        functools.partial(main_kernel, hop),
        [buffer(lon, rows, lat), buffer(5, lon, lev, lat)],
        [HBM] + [VMEM] * 2,
        [VMEM] * 2,
        [buffer(lon, rows, lat)],
        [lon],
    )(held[0], sent, coupling)
    z, coef = in_vmem(z), in_vmem(coef)
    out = jax.ShapeDtypeStruct(state.shape, f32)
    state, ze = call(
        functools.partial(sides_kernel, hop),
        [out, buffer(2, rows, lat)],
        [HBM] + [VMEM] * 7,
        [HBM, VMEM],
        [buffer(lon - 2, rows, lat)],
        [lon],
    )(held[0], packed, sent, coupling, near_x, far_x, z, coef)
    ze = in_vmem(ze)
    for i, size in enumerate(sizes):
        state = call(
            functools.partial(finish_kernel, hop, sum(sizes[:i])),
            out,
            [VMEM] * 4 + [HBM],
            HBM,
            [buffer(2, size, lat)],
            [2],
            {4: 0},
        )(near_p[i], far_p[i], ze, coef, in_hbm(state))
    return state


def per_device(forcing, trajectory, land_mask, coupling):
    _, mem, var, lev, lon, lat = forcing.shape
    assert lax.axis_size("space") % 2 == 0 and lon >= 3 and STEPS == 2
    state = forcing.reshape(mem * var * lev, lon, lat)
    for hop in range(lax.axis_size("tm") - 1):
        state = advance(hop, state, trajectory[0], land_mask, coupling)
    return state.reshape(forcing.shape)


def solution(mesh):
    return jax.shard_map(
        per_device,
        mesh=mesh,
        in_specs=(
            P("tm", None, None, None, "space", None),
            P("tm", None, None, "space", None),
            P(None, "space", None),
            P(),
        ),
        out_specs=P("tm", None, None, None, "space", None),
        check_vma=False,
    )
```
